256 devices in a mesh: proj: 64 (over y, z, core), grp: 4 (over x).
Axes of the slice: x: 4, y: 4, z: 8, core: 2. Of those that a mesh axis runs over, the one named last changes fastest.
Arguments:
- grads: bfloat16 [1024, 131072], P('grp', 'proj'), may hold values from -16 to 16
- proj_matrix: bfloat16 [131072, 8192], P('proj', 'grp'), may hold values from -48 to 48
- targets: bfloat16 [2048, 8192], P('proj', 'grp'), may hold values from -480 to 480
Outputs:
- scores: float32 [1024, 2048], P('proj', 'grp')
The draws below stay inside these ranges and needn't reach their ends.
All inputs are finite; a program needn't handle non-finite values.
Results may differ from the reference program's by a relative error of at most 0.0029.
Values may be sent and summed in bfloat16 or wider, within the bound.
A program may use at most 128 MiB of HBM per device.

```python
import jax
import jax.numpy as jnp
from jax import lax

K = 8192
EX = 1024
TGT = 2048
P_SIZE = 131072


def column_scales(key):
    inner_key = jax.random.fold_in(key, 7)
    spread = jax.random.uniform(inner_key, (K,), jnp.float32, -1.15, 1.15)
    ramp = jnp.power(3.0, jnp.arange(K, dtype=jnp.float32) / K)
    return ramp * jnp.exp(spread)


def draw_proj_matrix(key, part):
    scales = column_scales(key)
    inner_key = jax.random.fold_in(key, 11)
    values = jnp.clip(jax.random.normal(inner_key, (P_SIZE, K), jnp.float32), -5.0, 5.0)
    return (values * scales[None, :]).astype(jnp.bfloat16)


def draw_targets(key, part):
    scales = column_scales(key)
    inner_key = jax.random.fold_in(key, 13)
    row_key = jax.random.fold_in(key, 17)
    row_scales = jnp.exp(jax.random.uniform(row_key, (TGT,), jnp.float32, 0.0, 2.3))
    values = jnp.clip(jax.random.normal(inner_key, (TGT, K), jnp.float32), -5.0, 5.0)
    return (values * scales[None, :] * row_scales[:, None]).astype(jnp.bfloat16)


def strengthened(array, stream_key, source, target, shards_of, factor):
    owner, partner = [(jnp.arange(array.shape[dim]) // (array.shape[dim] // shards_of)).reshape([-1 if axis == dim else 1 for axis in range(array.ndim)]) for dim in (source, target)]
    chosen = jax.random.permutation(stream_key, shards_of)[partner]
    strong = (owner == chosen) | (owner == (partner + shards_of // 2) % shards_of)
    return jnp.where(strong, factor * array, array)


def levels(stream_key, shape, cuts, smallest, high):
    def one(position, parts):
        steps = jax.random.uniform(jax.random.fold_in(jax.random.fold_in(stream_key, 6), position), (parts,), jnp.float32, smallest / len(cuts), high / len(cuts))
        return jnp.repeat(jnp.exp(steps), shape[position] // parts).reshape((-1,) + (1,) * (len(shape) - position - 1))

    gain = one(*cuts[0])
    for cut in cuts[1:]:
        gain = gain * one(*cut)
    return gain


def bell_draw_with(own_key, extent, width, most, shards, heavy, kind=jnp.bfloat16):
    values = width * jax.random.normal(own_key, extent, jnp.float32)
    if shards:
        values = values * levels(own_key, extent, shards, -0.22, 0.18)
    return jnp.clip(strengthened(values, jax.random.fold_in(own_key, 3), *heavy), -most, most).astype(kind)


def setup_inputs(seed: int = 0) -> dict:
    key_of = jax.random.split(jax.random.key(seed), 4)
    return {
        "grads": bell_draw_with(key_of[0], (EX, P_SIZE), 1.0, 16.0, ((0, 4), (1, 64)), (1, 0, 64, 4.0)),
        "proj_matrix": draw_proj_matrix(jax.random.fold_in(key_of[3], 71), 0),
        "targets": draw_targets(jax.random.fold_in(key_of[3], 71), 0),
    }


def reference(grads, proj_matrix, targets):
    features = jnp.dot(grads, proj_matrix, preferred_element_type=jnp.float32)
    rounded = features.astype(jnp.bfloat16)
    feature_sq = lax.optimization_barrier(jnp.sum(jnp.square(rounded.astype(jnp.float32)), axis=1))
    target_sq = lax.optimization_barrier(jnp.sum(jnp.square(targets.astype(jnp.float32)), axis=1))
    products = lax.dot_general(rounded, targets, (((1,), (1,)), ((), ())), preferred_element_type=jnp.float32)
    factor = float(K) ** 0.5
    return factor * products * lax.rsqrt(feature_sq + 1e-06)[:, None] * lax.rsqrt(target_sq + 1e-06)[None, :]
```

```python
import jax
import jax.numpy as jnp
from jax import lax
from jax.experimental import pallas as pl
from jax.experimental.pallas import tpu as pltpu
from jax.sharding import PartitionSpec as P

K = 8192
MESH = pl.DeviceIdType.MESH
NX, NY, NZ, NC = 4, 4, 8, 2
CH, RC, RZ = 4, 64, 8
COLS = 512
LANES = COLS + 256


def kernel(
    g_ref, m_ref, t_ref, out_ref,
    gb, mb, fp, yr, zb, zr, fz, fb, tb, tq, pb, xr, sb, fr,
    loc_sem, gs, gr, ss, sr, ms, mr, ts, tr, tzs, tzr, ys, yrs, zs, zrs, fs, frs, xs, xrs, es, ers,
):
    x = lax.axis_index("grp")
    p = lax.axis_index("proj")
    c = p % NC
    z = (p // NC) % NZ
    y = p // (NC * NZ)
    depth = m_ref.shape[0]
    half = m_ref.shape[1] // NC
    trows = t_ref.shape[0]
    sib = 1 - c

    def dev(dx, dy, dz, dc):
        return ((dy * NZ + dz) * NC + dc, dx)

    here = dev(x, y, z, c)
    right, left = (x + 1) % NX, (x + NX - 1) % NX
    across = (x + 2) % NX

    def remote(src, dst, send, recv, where):
        return pltpu.make_async_remote_copy(
            src_ref=src, dst_ref=dst, send_sem=send, recv_sem=recv,
            device_id=where, device_id_type=MESH,
        )

    def arrived(dst, sem):
        remote(dst, dst, sem, sem, dev(x, y, z, sib)).wait_recv()

    def sent(src, sem):
        remote(src, src, sem, sem, dev(x, y, z, sib)).wait_send()

    own_cols = pl.ds(pl.multiple_of(c * half, half), half)
    sib_cols = pl.ds(pl.multiple_of(sib * half, half), half)
    own_t = tb.at[z, pl.ds(pl.multiple_of(c * trows, trows), trows), :]
    sib_t = tb.at[z, pl.ds(pl.multiple_of(sib * trows, trows), trows), :]

    local = []
    for k in range(CH):
        local.append(pltpu.make_async_copy(
            g_ref.at[pl.ds(k * RC, RC), :], gb.at[0, k, x], loc_sem.at[k]))
    local.append(pltpu.make_async_copy(t_ref.at[:, own_cols], own_t, loc_sem.at[CH]))
    local.append(pltpu.make_async_copy(m_ref.at[:, own_cols], mb.at[0], loc_sem.at[CH + 1]))
    for copy in local:
        copy.start()

    barrier = pltpu.get_barrier_semaphore()
    zo = z // 4
    co = (z // 2) % 2
    for d in range(1, NX):
        pl.semaphore_signal(barrier, inc=1, device_id=dev((x + d) % NX, y, z, c), device_id_type=MESH)
    pl.semaphore_signal(barrier, inc=1, device_id=dev(x, y, z, sib), device_id_type=MESH)
    for d in range(1, NY):
        pl.semaphore_signal(barrier, inc=1, device_id=dev(x, (y + d) % NY, z, c), device_id_type=MESH)
    for d in range(1, NZ):
        pl.semaphore_signal(barrier, inc=1, device_id=dev(x, y, (z + d) % NZ, c), device_id_type=MESH)
    for zp in range(2):
        for cp in range(NC):
            zf = 4 * (z % 2) + 2 * c + zp
            pl.semaphore_signal(barrier, inc=1, device_id=dev(y, x, zf, cp), device_id_type=MESH)
    pl.semaphore_wait(barrier, (NX - 1) + 1 + (NY - 1) + (NZ - 1) + 4)

    def own_sends(k):
        src = g_ref.at[pl.ds(k * RC, RC), :]
        dst = gb.at[0, k, x]
        return [
            remote(src, dst, gs.at[k, 0], gr.at[k, 0], dev(right, y, z, c)),
            remote(src, dst, gs.at[k, 1], gr.at[k, 1], dev(left, y, z, c)),
            remote(src, gb.at[1, k, x], ss.at[k, 0], sr.at[k, 0], dev(x, y, z, sib)),
        ]

    def to_sibling(k, who, slot):
        return remote(gb.at[0, k, who], gb.at[1, k, who], ss.at[k, slot], sr.at[k, slot], dev(x, y, z, sib))

    started = []

    def go(copies):
        for copy in copies:
            copy.start()
            started.append(copy)

    go(own_sends(0))
    go([remote(t_ref.at[:, sib_cols], own_t, ts, tr, dev(x, y, z, sib))])
    go([remote(m_ref.at[:, sib_cols], mb.at[1], ms, mr, dev(x, y, z, sib))])
    go(own_sends(1))

    local[CH].wait()
    arrived(sib_t, tr)
    for d in range(1, NZ):
        go([remote(tb.at[z], tb.at[z], tzs.at[d - 1], tzr.at[d - 1], dev(x, y, (z + d) % NZ, c))])

    def product(k):
        @pl.loop(0, half // 256)
        def _(n):
            cols = pl.ds(pl.multiple_of(n * 256, 256), 256)
            acc = jnp.dot(
                gb[0, k].reshape(NX * RC, depth), mb[0, :, cols], preferred_element_type=jnp.float32)
            acc = acc + jnp.dot(
                gb[1, k].reshape(NX * RC, depth), mb[1, :, cols], preferred_element_type=jnp.float32)
            fp[k, :, :, cols] = acc.reshape(NY, RC, 256)

    def y_stage(k):
        for d in range(1, NY):
            go([remote(fp.at[k, (y + d) % NY], yr.at[k, d - 1], ys.at[k, d - 1], yrs.at[k, d - 1],
                       dev(x, (y + d) % NY, z, c))])

    def z_stage(k):
        for d in range(1, NY):
            arrived(yr.at[k, d - 1], yrs.at[k, d - 1])
        zb[k] = (fp[k, y] + yr[k, 0]) + (yr[k, 1] + yr[k, 2])
        for d in range(1, NZ):
            to = (z + d) % NZ
            go([remote(zb.at[k, pl.ds(pl.multiple_of(to * RZ, RZ), RZ), :], zr.at[k, d - 1],
                       zs.at[k, d - 1], zrs.at[k, d - 1], dev(x, y, to, c))])

    def z_sum(k):
        for d in range(1, NZ):
            arrived(zr.at[k, d - 1], zrs.at[k, d - 1])
        total = zb[k, pl.ds(pl.multiple_of(z * RZ, RZ), RZ), :]
        for d in range(1, NZ):
            total = total + zr[k, d - 1]
        fz[k] = total

    for k in range(CH):
        h = RC // 2
        arrived(gb.at[0, k, left], gr.at[k, 0])
        go([remote(gb.at[0, k, left, pl.ds(0, h), :], gb.at[0, k, left, pl.ds(0, h), :],
                   gs.at[k, 2], gr.at[k, 2], dev(right, y, z, c)),
            to_sibling(k, left, 1)])
        arrived(gb.at[0, k, right], gr.at[k, 1])
        go([remote(gb.at[0, k, right, pl.ds(h, h), :], gb.at[0, k, right, pl.ds(h, h), :],
                   gs.at[k, 3], gr.at[k, 3], dev(left, y, z, c)),
            to_sibling(k, right, 2)])
        if k + 2 < CH:
            go(own_sends(k + 2))
        if k >= 1:
            z_stage(k - 1)
        if k >= 2:
            z_sum(k - 2)
        if k == CH - 1:
            for d in range(1, NZ):
                arrived(tb.at[(z + NZ - d) % NZ], tzr.at[d - 1])
            ones = jnp.ones((8, half), jnp.bfloat16)
            tq[...] = jnp.zeros_like(tq)
            for j in range(COLS // 128):
                sq = jnp.square(tb[pl.ds(2 * j, 2)].reshape(128, half).astype(jnp.float32))
                high = sq.astype(jnp.bfloat16)
                low = (sq - high.astype(jnp.float32)).astype(jnp.bfloat16)
                row = inner_rows(ones, high) + inner_rows(ones, low)
                tq[j:j + 1, :] = row[0:1, :]
        arrived(gb.at[0, k, across, pl.ds(0, h), :], gr.at[k, 2])
        arrived(gb.at[0, k, across, pl.ds(h, h), :], gr.at[k, 3])
        go([to_sibling(k, across, 3)])
        local[k].wait()
        if k == 0:
            local[CH + 1].wait()
            arrived(mb.at[1], mr)
        arrived(gb.at[1, k, x], sr.at[k, 0])
        arrived(gb.at[1, k, left], sr.at[k, 1])
        arrived(gb.at[1, k, right], sr.at[k, 2])
        arrived(gb.at[1, k, across], sr.at[k, 3])
        product(k)
        y_stage(k)

    z_sum(CH - 2)
    z_stage(CH - 1)
    z_sum(CH - 1)
    fb[y] = fz[...].reshape(CH * RZ, half).astype(jnp.bfloat16)

    for d in range(1, NY):
        go([remote(fb.at[y], fb.at[y], fs.at[d - 1], frs.at[d - 1], dev(x, (y + d) % NY, z, c))])
    for d in range(1, NY):
        arrived(fb.at[(y + NY - d) % NY], frs.at[d - 1])
    rows = fb[...].reshape(NY * CH * RZ, half)
    pb[:, :, 0:COLS] = inner_rows(rows, tb[...].reshape(COLS, half)).reshape(NY, CH * RZ, COLS)
    sq = jnp.sum(jnp.square(rows.astype(jnp.float32)), axis=1, keepdims=True)
    pb[:, :, COLS:COLS + 128] = jnp.broadcast_to(sq, (NY * CH * RZ, 128)).reshape(NY, CH * RZ, 128)
    quarter = tq[...]
    for b in range(NY):
        for k in range(CH):
            pb[b, k * RZ:(k + 1) * RZ, COLS + 128:] = quarter

    for d in range(1, NX):
        go([remote(pb.at[(x + d) % NX], xr.at[d - 1], xs.at[d - 1], xrs.at[d - 1],
                   dev((x + d) % NX, y, z, c))])
    for d in range(1, NX):
        arrived(xr.at[d - 1], xrs.at[d - 1])
    sb[...] = ((pb[x] + xr[0]) + (xr[1] + xr[2])).reshape(CH, RZ, LANES)

    for k in range(CH):
        to = 2 * k + zo
        same = (x == y) & (to == z) & (c == co)

        @pl.when(same)
        def _():
            copy = pltpu.make_async_copy(sb.at[k], fr.at[z % 2, c], ers.at[z % 2, c])
            copy.start()

        @pl.when(jnp.logical_not(same))
        def _():
            copy = remote(sb.at[k], fr.at[z % 2, c], es.at[k], ers.at[z % 2, c], dev(y, x, to, co))
            copy.start()
            copy.wait_send()

    for zp in range(2):
        for cp in range(NC):
            arrived(fr.at[zp, cp], ers.at[zp, cp])
        m = fr[zp, 0] + fr[zp, 1]
        tsq = jnp.concatenate([m[j:j + 1, COLS + 128:] for j in range(COLS // 128)], axis=1)
        out_ref[zp * RZ:(zp + 1) * RZ, :] = (
            float(K) ** 0.5
            * m[:, 0:COLS]
            * lax.rsqrt(m[:, COLS:COLS + 1] + 1e-06)
            * lax.rsqrt(tsq + 1e-06)
        )

    for copy in started:
        copy.wait_send()


def inner_rows(left, right):
    return lax.dot_general(
        left, right, (((1,), (1,)), ((), ())), preferred_element_type=jnp.float32
    )


def per_device(grads, proj_matrix, targets):
    depth, dims = proj_matrix.shape
    half = dims // NC
    dma = pltpu.SemaphoreType.DMA
    bf16, f32 = jnp.bfloat16, jnp.float32
    return pl.pallas_call(
        kernel,
        out_shape=jax.ShapeDtypeStruct((2 * RZ, COLS), f32),
        in_specs=[pl.BlockSpec(memory_space=pltpu.HBM)] * 3,
        out_specs=pl.BlockSpec(memory_space=pltpu.VMEM),
        scratch_shapes=[
            pltpu.VMEM((NC, CH, NX, RC, depth), bf16),
            pltpu.VMEM((NC, depth, half), bf16),
            pltpu.VMEM((CH, NY, RC, half), f32),
            pltpu.VMEM((CH, NY - 1, RC, half), f32),
            pltpu.VMEM((CH, RC, half), f32),
            pltpu.VMEM((CH, NZ - 1, RZ, half), f32),
            pltpu.VMEM((CH, RZ, half), f32),
            pltpu.VMEM((NY, CH * RZ, half), bf16),
            pltpu.VMEM((NZ, NC * targets.shape[0], half), bf16),
            pltpu.VMEM((8, 128), f32),
            pltpu.VMEM((NY, CH * RZ, LANES), f32),
            pltpu.VMEM((NX - 1, CH * RZ, LANES), f32),
            pltpu.VMEM((CH, RZ, LANES), f32),
            pltpu.VMEM((2, NC, RZ, LANES), f32),
            dma((CH + 2,)),
            dma((CH, 4)), dma((CH, 4)), dma((CH, 4)), dma((CH, 4)),
            dma, dma, dma, dma,
            dma((NZ - 1,)), dma((NZ - 1,)),
            dma((CH, NY - 1)), dma((CH, NY - 1)),
            dma((CH, NZ - 1)), dma((CH, NZ - 1)),
            dma((NY - 1,)), dma((NY - 1,)),
            dma((NX - 1,)), dma((NX - 1,)),
            dma((CH,)), dma((2, NC)),
        ],
        compiler_params=pltpu.CompilerParams(
            collective_id=0, has_side_effects=True, vmem_limit_bytes=56 * 1024 * 1024
        ),
    )(grads, proj_matrix, targets)


def solution(mesh):
    placed = (P("grp", "proj"), P("proj", "grp"), P("proj", "grp"))
    return jax.shard_map(
        per_device, mesh=mesh, in_specs=placed, out_specs=P("proj", "grp"), check_vma=False
    )
```

```python
import jax
import jax.numpy as jnp
from jax import lax
from jax.experimental import pallas as pl
from jax.experimental.pallas import tpu as pltpu
from jax.sharding import PartitionSpec as P

K = 8192
MESH = pl.DeviceIdType.MESH
NX, NY, NZ, NC = 4, 4, 8, 2
CH, RC, RZ, HP = 4, 64, 8, 2
COLS = 512
LANES = COLS + 256


def inner_rows(left, right):
    return lax.dot_general(
        left, right, (((1,), (1,)), ((), ())), preferred_element_type=jnp.float32
    )


def kernel(
    g_ref, m_ref, t_ref, out_ref,
    gb, mb, fo, fp, yr, zb, zr, fb, tb, tq, pb, fr,
    gl, loc, gs, gr, ss, sr, ms, mr, ts, tr, tzs, tzr, ys, yrs, zs, zrs, fs, frs, es, ers,
):
    x = lax.axis_index("grp")
    p = lax.axis_index("proj")
    c = p % NC
    z = (p // NC) % NZ
    y = p // (NC * NZ)
    depth = m_ref.shape[0]
    half = m_ref.shape[1] // NC
    part = half // HP
    trows = t_ref.shape[0]
    sib = 1 - c

    def dev(dx, dy, dz, dc):
        return ((dy * NZ + dz) * NC + dc, dx)

    right, left = (x + 1) % NX, (x + NX - 1) % NX
    across = (x + 2) % NX

    def remote(src, dst, send, recv, where):
        return pltpu.make_async_remote_copy(
            src_ref=src, dst_ref=dst, send_sem=send, recv_sem=recv,
            device_id=where, device_id_type=MESH,
        )

    def arrived(dst, sem):
        remote(dst, dst, sem, sem, dev(x, y, z, sib)).wait_recv()

    own_cols = pl.ds(pl.multiple_of(c * half, half), half)
    sib_cols = pl.ds(pl.multiple_of(sib * half, half), half)
    own_t = tb.at[z, pl.ds(pl.multiple_of(c * trows, trows), trows), :]
    sib_t = tb.at[z, pl.ds(pl.multiple_of(sib * trows, trows), trows), :]

    g_local = []
    for k in range(CH):
        g_local.append([
            pltpu.make_async_copy(
                g_ref.at[pl.ds(w * CH * RZ + k * RZ, RZ), :],
                gb.at[0, k, x, pl.ds(w * RZ, RZ), :], gl.at[k, w])
            for w in range(NZ)
        ])
    t_local = pltpu.make_async_copy(t_ref.at[:, own_cols], own_t, loc.at[0])
    m_local = pltpu.make_async_copy(m_ref.at[:, own_cols], mb.at[0], loc.at[1])
    for k in range(CH):
        for copy in g_local[k]:
            copy.start()
        if k == 0:
            t_local.start()
    m_local.start()

    barrier = pltpu.get_barrier_semaphore()

    def greet(where):
        pl.semaphore_signal(barrier, inc=1, device_id=where, device_id_type=MESH)

    for xs in range(NX):
        for cs in range(NC):
            greet(dev(xs, x, z, cs))
    for d in range(1, NZ):
        greet(dev(x, y, (z + d) % NZ, c))
    for d in range(1, NY):
        greet(dev(x, (y + d) % NY, z, c))
    greet(dev(right, y, z, c))
    greet(dev(left, y, z, c))
    greet(dev(x, y, z, sib))
    pl.semaphore_wait(barrier, NX * NC + (NZ - 1) + (NY - 1) + 3)

    started = []

    def go(copies):
        for copy in copies:
            copy.start()
            started.append(copy)

    def to_sibling(k, who, slot):
        return remote(gb.at[0, k, who], gb.at[1, k, who], ss.at[k, slot], sr.at[k, slot], dev(x, y, z, sib))

    def own_sends(k):
        for copy in g_local[k]:
            copy.wait()
        block = gb.at[0, k, x]
        go([
            remote(block, block, gs.at[k, 0], gr.at[k, 0], dev(right, y, z, c)),
            remote(block, block, gs.at[k, 1], gr.at[k, 1], dev(left, y, z, c)),
            to_sibling(k, x, 0),
        ])

    own_sends(0)
    go([remote(t_ref.at[:, sib_cols], own_t, ts, tr, dev(x, y, z, sib))])
    go([remote(m_ref.at[:, sib_cols], mb.at[1], ms, mr, dev(x, y, z, sib))])
    own_sends(1)

    t_local.wait()
    arrived(sib_t, tr)
    for d in range(1, NZ):
        go([remote(tb.at[z], tb.at[z], tzs.at[d - 1], tzr.at[d - 1], dev(x, y, (z + d) % NZ, c))])

    def product(k, h):
        @pl.loop(0, part // 256)
        def _(n):
            first = pl.multiple_of(n * 256, 256)
            cols = pl.ds(h * part + first, 256)
            acc = jnp.dot(
                gb[0, k].reshape(NX * RC, depth), mb[0, :, cols], preferred_element_type=jnp.float32)
            acc = acc + jnp.dot(
                gb[1, k].reshape(NX * RC, depth), mb[1, :, cols], preferred_element_type=jnp.float32)
            acc = acc.reshape(NY, RC, 256)
            fo[k, h, :, :, pl.ds(first, 256)] = acc
            fp[k, h, :, :, pl.ds(first, 256)] = acc.astype(jnp.bfloat16)

    def y_send(k, h):
        for d in range(1, NY):
            to = (y + d) % NY
            go([remote(fp.at[k, h, to], yr.at[k, h, d - 1], ys.at[k, h, d - 1], yrs.at[k, h, d - 1],
                       dev(x, to, z, c))])

    def z_stage(k, h):
        for d in range(1, NY):
            arrived(yr.at[k, h, d - 1], yrs.at[k, h, d - 1])
        total = fo[k, h, y]
        for d in range(1, NY):
            total = total + yr[k, h, d - 1].astype(jnp.float32)
        zb[k, h] = total
        for d in range(1, NZ):
            to = (z + d) % NZ
            go([remote(zb.at[k, h, pl.ds(pl.multiple_of(to * RZ, RZ), RZ), :], zr.at[k, h, d - 1],
                       zs.at[k, h, d - 1], zrs.at[k, h, d - 1], dev(x, y, to, c))])

    def z_sum(k):
        for h in range(HP):
            for d in range(1, NZ):
                arrived(zr.at[k, h, d - 1], zrs.at[k, h, d - 1])
            total = zb[k, h, pl.ds(pl.multiple_of(z * RZ, RZ), RZ), :]
            for d in range(1, NZ):
                total = total + zr[k, h, d - 1]
            fb[k, y, :, h * part:(h + 1) * part] = total
        for d in range(1, NY):
            to = (y + d) % NY
            go([remote(fb.at[k, y], fb.at[k, y], fs.at[k, d - 1], frs.at[k, d - 1], dev(x, to, z, c))])

    def target_squares():
        for d in range(1, NZ):
            arrived(tb.at[(z + NZ - d) % NZ], tzr.at[d - 1])
        ones = jnp.ones((8, half), jnp.bfloat16)
        tq[...] = jnp.zeros_like(tq)
        for j in range(COLS // 128):
            sq = jnp.square(tb[pl.ds(2 * j, 2)].reshape(128, half).astype(jnp.float32))
            high = sq.astype(jnp.bfloat16)
            low = (sq - high.astype(jnp.float32)).astype(jnp.bfloat16)
            row = inner_rows(ones, high) + inner_rows(ones, low)
            tq[j:j + 1, :] = row[0:1, :]

    def owner_copy(k, d):
        to = (y + d) % NY
        cc, hh = k // 2, k % 2
        return remote(pb.at[k, to], fr.at[hh, x, c], es.at[k, d], ers.at[hh, x, c], dev(y, to, z, cc))

    def scores(k):
        for d in range(1, NY):
            arrived(fb.at[k, (y + NY - d) % NY], frs.at[k, d - 1])
        rows = fb[k].reshape(NY * RZ, half)
        high = rows.astype(jnp.bfloat16)
        low = (rows - high.astype(jnp.float32)).astype(jnp.bfloat16)
        both = inner_rows(jnp.concatenate([high, low], axis=0), tb[...].reshape(COLS, half))
        pb[k, :, :, 0:COLS] = (both[:NY * RZ] + both[NY * RZ:]).reshape(NY, RZ, COLS)
        sq = jnp.sum(jnp.square(rows), axis=1, keepdims=True)
        pb[k, :, :, COLS:COLS + 128] = jnp.broadcast_to(sq, (NY * RZ, 128)).reshape(NY, RZ, 128)
        pb[k, :, :, COLS + 128:] = jnp.broadcast_to(tq[...][None], (NY, RZ, 128))
        same = (x == y) & (c == k // 2)

        @pl.when(same)
        def _():
            pltpu.make_async_copy(pb.at[k, y], fr.at[k % 2, x, c], ers.at[k % 2, x, c]).start()

        @pl.when(jnp.logical_not(same))
        def _():
            owner_copy(k, 0).start()

        for d in range(1, NY):
            go([owner_copy(k, d)])

    h = RC // 2
    for k in range(CH):
        arrived(gb.at[0, k, left], gr.at[k, 0])
        go([remote(gb.at[0, k, left, pl.ds(0, h), :], gb.at[0, k, left, pl.ds(0, h), :],
                   gs.at[k, 2], gr.at[k, 2], dev(right, y, z, c)),
            to_sibling(k, left, 1)])
        arrived(gb.at[0, k, right], gr.at[k, 1])
        go([remote(gb.at[0, k, right, pl.ds(h, h), :], gb.at[0, k, right, pl.ds(h, h), :],
                   gs.at[k, 3], gr.at[k, 3], dev(left, y, z, c)),
            to_sibling(k, right, 2)])
        if k + 2 < CH:
            own_sends(k + 2)
        if k >= 1:
            z_stage(k - 1, 0)
            z_stage(k - 1, 1)
        if k >= 2:
            z_sum(k - 2)
        if k == CH - 1:
            target_squares()
            scores(k - 3)
        arrived(gb.at[0, k, across, pl.ds(0, h), :], gr.at[k, 2])
        arrived(gb.at[0, k, across, pl.ds(h, h), :], gr.at[k, 3])
        go([to_sibling(k, across, 3)])
        if k == 0:
            m_local.wait()
            arrived(mb.at[1], mr)
        arrived(gb.at[1, k, x], sr.at[k, 0])
        arrived(gb.at[1, k, left], sr.at[k, 1])
        arrived(gb.at[1, k, right], sr.at[k, 2])
        arrived(gb.at[1, k, across], sr.at[k, 3])
        for q in range(HP):
            product(k, q)
            y_send(k, q)

    z_sum(CH - 2)
    scores(CH - 3)
    z_stage(CH - 1, 0)
    z_stage(CH - 1, 1)
    scores(CH - 2)
    z_sum(CH - 1)
    scores(CH - 1)

    for hh in range(2):
        m = None
        for xs in range(NX):
            for cs in range(NC):
                arrived(fr.at[hh, xs, cs], ers.at[hh, xs, cs])
        m = fr[hh, 0, 0]
        for s in range(1, NX * NC):
            m = m + fr[hh, s // NC, s % NC]
        tsq = jnp.concatenate([m[j:j + 1, COLS + 128:] for j in range(COLS // 128)], axis=1)
        out_ref[hh * RZ:(hh + 1) * RZ, :] = (
            float(K) ** 0.5
            * m[:, 0:COLS]
            * lax.rsqrt(m[:, COLS:COLS + 1] + 1e-06)
            * lax.rsqrt(tsq + 1e-06)
        )

    for copy in started:
        copy.wait_send()
    for k in range(CH):
        @pl.when(jnp.logical_not((x == y) & (c == k // 2)))
        def _():
            owner_copy(k, 0).wait_send()


def per_device(grads, proj_matrix, targets):
    depth, dims = proj_matrix.shape
    half = dims // NC
    part = half // HP
    dma = pltpu.SemaphoreType.DMA
    bf16, f32 = jnp.bfloat16, jnp.float32
    return pl.pallas_call(
        kernel,
        out_shape=jax.ShapeDtypeStruct((2 * RZ, COLS), f32),
        in_specs=[pl.BlockSpec(memory_space=pltpu.HBM)] * 3,
        out_specs=pl.BlockSpec(memory_space=pltpu.VMEM),
        scratch_shapes=[
            pltpu.VMEM((NC, CH, NX, RC, depth), bf16),
            pltpu.VMEM((NC, depth, half), bf16),
            pltpu.VMEM((CH, HP, NY, RC, part), f32),
            pltpu.VMEM((CH, HP, NY, RC, part), bf16),
            pltpu.VMEM((CH, HP, NY - 1, RC, part), bf16),
            pltpu.VMEM((CH, HP, RC, part), f32),
            pltpu.VMEM((CH, HP, NZ - 1, RZ, part), f32),
            pltpu.VMEM((CH, NY, RZ, half), f32),
            pltpu.VMEM((NZ, NC * targets.shape[0], half), bf16),
            pltpu.VMEM((8, 128), f32),
            pltpu.VMEM((CH, NY, RZ, LANES), f32),
            pltpu.VMEM((2, NX, NC, RZ, LANES), f32),
            dma((CH, NZ)), dma((2,)),
            dma((CH, 4)), dma((CH, 4)), dma((CH, 4)), dma((CH, 4)),
            dma, dma, dma, dma,
            dma((NZ - 1,)), dma((NZ - 1,)),
            dma((CH, HP, NY - 1)), dma((CH, HP, NY - 1)),
            dma((CH, HP, NZ - 1)), dma((CH, HP, NZ - 1)),
            dma((CH, NY - 1)), dma((CH, NY - 1)),
            dma((CH, NY)), dma((2, NX, NC)),
        ],
        compiler_params=pltpu.CompilerParams(
            collective_id=0, has_side_effects=True, vmem_limit_bytes=56 * 1024 * 1024
        ),
    )(grads, proj_matrix, targets)


def solution(mesh):
    placed = (P("grp", "proj"), P("proj", "grp"), P("proj", "grp"))
    return jax.shard_map(
        per_device, mesh=mesh, in_specs=placed, out_specs=P("proj", "grp"), check_vma=False
    )
```

```python
import jax
import jax.numpy as jnp
from jax import lax
from jax.experimental import pallas as pl
from jax.experimental.pallas import tpu as pltpu
from jax.sharding import PartitionSpec as P

K = 8192
MESH = pl.DeviceIdType.MESH
NX, NY, NZ, NC = 4, 4, 8, 2
CH, RC, RZ, HP = 4, 64, 8, 2
COLS, TILE = 512, 128


def inner_rows(left, right):
    return lax.dot_general(
        left, right, (((1,), (1,)), ((), ())), preferred_element_type=jnp.float32
    )


def kernel(
    g_ref, m_ref, t_ref, out_ref,
    gb, mb, fo, fp, yr, zb, zq, zr, zt, fb, tb, order, pb, fr,
    gl, loc, gs, gr, ss, sr, ms, mr, ts, tr, tzs, tzr, ys, yrs, zs, zrs, fs, frs, es, ers,
):
    x = lax.axis_index("grp")
    p = lax.axis_index("proj")
    c = p % NC
    z = (p // NC) % NZ
    y = p // (NC * NZ)
    depth = m_ref.shape[0]
    half = m_ref.shape[1] // NC
    part = half // HP
    sib = 1 - c

    def dev(dx, dy, dz, dc):
        return ((dy * NZ + dz) * NC + dc, dx)

    right, left = (x + 1) % NX, (x + NX - 1) % NX
    across = (x + 2) % NX

    def remote(src, dst, send, recv, where):
        return pltpu.make_async_remote_copy(
            src_ref=src, dst_ref=dst, send_sem=send, recv_sem=recv,
            device_id=where, device_id_type=MESH,
        )

    def arrived(dst, sem):
        remote(dst, dst, sem, sem, dev(x, y, z, sib)).wait_recv()

    own_cols = pl.ds(pl.multiple_of(c * half, half), half)
    sib_cols = pl.ds(pl.multiple_of(sib * half, half), half)
    g_local = []
    for k in range(CH):
        g_local.append([
            pltpu.make_async_copy(
                g_ref.at[pl.ds(w * CH * RZ + k * RZ, RZ), :],
                gb.at[0, k, x, pl.ds(w * RZ, RZ), :], gl.at[k, w])
            for w in range(NZ)
        ])
    m_local = pltpu.make_async_copy(m_ref.at[:, own_cols], mb.at[0], loc.at[1])
    for k in range(CH):
        for copy in g_local[k]:
            copy.start()
    m_local.start()

    barrier = pltpu.get_barrier_semaphore()

    def greet(where):
        pl.semaphore_signal(barrier, inc=1, device_id=where, device_id_type=MESH)

    for dx in range(NX):
        for dy in range(NY):
            for cs in range(NC):
                greet(dev((x + dx) % NX, (y + dy) % NY, z, cs))
    for d in range(1, NZ):
        greet(dev(x, y, (z + d) % NZ, c))
    pl.semaphore_wait(barrier, NX * NY * NC + NZ - 1)

    started = []

    def go(copies):
        for copy in copies:
            copy.start()
            started.append(copy)

    def to_sibling(k, who, slot):
        return remote(gb.at[0, k, who], gb.at[1, k, who], ss.at[k, slot], sr.at[k, slot], dev(x, y, z, sib))

    def rows_of(k, who, which):
        return gb.at[0, k, who, pl.ds(which * (RC // 2), RC // 2), :]

    def own_sends(k):
        for copy in g_local[k]:
            copy.wait()
        first, last = rows_of(k, x, 0), rows_of(k, x, 1)
        go([
            remote(first, first, gs.at[k, 0], gr.at[k, 0], dev(right, y, z, c)),
            remote(last, last, gs.at[k, 2], gr.at[k, 2], dev(left, y, z, c)),
            remote(last, last, gs.at[k, 1], gr.at[k, 1], dev(right, y, z, c)),
            remote(first, first, gs.at[k, 3], gr.at[k, 3], dev(left, y, z, c)),
            to_sibling(k, x, 0),
        ])

    own_sends(0)
    trows = t_ref.shape[0] // HP

    def deal(j, cc):
        source = t_ref.at[pl.ds(j * trows, trows), pl.ds(cc * half, half)]
        to = HP * c + j
        same = (to == y) & (cc == c)
        return same, remote(source, tb.at[y, z], ts.at[j, cc], tr, dev(x, to, z, cc)), source

    for j in range(HP):
        for cc in range(NC):
            same, copy, source = deal(j, cc)

            @pl.when(same)
            def _():
                pltpu.make_async_copy(source, tb.at[y, z], tr).start()

            @pl.when(jnp.logical_not(same))
            def _():
                copy.start()

    go([remote(m_ref.at[:, sib_cols], mb.at[1], ms, mr, dev(x, y, z, sib))])
    own_sends(1)

    arrived(tb.at[:, z], tr)
    for d in range(1, NZ):
        go([remote(tb.at[:, z], tb.at[:, z], tzs.at[d - 1], tzr.at[d - 1], dev(x, y, (z + d) % NZ, c))])

    def own_product(k):
        @pl.loop(0, half // 256)
        def _(n):
            cols = pl.ds(pl.multiple_of(n * 256, 256), 256)
            acc = jnp.dot(
                gb[0, k].reshape(NX * RC, depth), mb[0, :, cols], preferred_element_type=jnp.float32)
            fo[k, n // (part // 256), :, :, pl.ds(pl.multiple_of(n % (part // 256) * 256, 256), 256)] = (
                acc.reshape(NY, RC, 256))

    def sibling_product(k, h):
        @pl.loop(0, part // 256)
        def _(n):
            first = pl.multiple_of(n * 256, 256)
            cols = pl.ds(h * part + first, 256)
            acc = jnp.dot(
                gb[1, k].reshape(NX * RC, depth), mb[1, :, cols], preferred_element_type=jnp.float32)
            acc = fo[k, h, :, :, pl.ds(first, 256)] + acc.reshape(NY, RC, 256)
            fo[k, h, :, :, pl.ds(first, 256)] = acc
            fp[k, h, :, :, pl.ds(first, 256)] = acc.astype(jnp.bfloat16)

    def y_send(k, h):
        for d in range(1, NY):
            to = (y + d) % NY
            go([remote(fp.at[k, h, to], yr.at[k, h, d - 1], ys.at[k, h, d - 1], yrs.at[k, h, d - 1],
                       dev(x, to, z, c))])

    def z_slot(k, h, d):
        return zt.at[h, d - 1] if k == CH - 1 else zr.at[k, h, d - 1]

    def z_stage(k, h):
        for d in range(1, NY):
            arrived(yr.at[k, h, d - 1], yrs.at[k, h, d - 1])
        total = fo[k, h, y]
        for d in range(1, NY):
            total = total + yr[k, h, d - 1].astype(jnp.float32)
        zb[k, h] = total
        source = zb.at[k, h]
        if k == CH - 1:
            zq[h] = total.astype(jnp.bfloat16)
            source = zq.at[h]
        for d in range(1, NZ):
            to = (z + d) % NZ
            piece = pl.ds(pl.multiple_of(to * RZ, RZ), RZ)
            go([remote(source.at[piece, :], z_slot(k, h, d),
                       zs.at[k, h, d - 1], zrs.at[k, h, d - 1], dev(x, y, to, c))])

    def z_sum(k):
        for h in range(HP):
            for d in range(1, NZ):
                arrived(z_slot(k, h, d), zrs.at[k, h, d - 1])
            total = zb[k, h, pl.ds(pl.multiple_of(z * RZ, RZ), RZ), :]
            for d in range(1, NZ):
                total = total + z_slot(k, h, d)[...].astype(jnp.float32)
            fb[k, y, :, h * part:(h + 1) * part] = total
        for d in range(1, NY):
            to = (y + d) % NY
            go([remote(fb.at[k, y], fb.at[k, y], fs.at[k, d - 1], frs.at[k, d - 1], dev(x, to, z, c))])

    def target_squares():
        for d in range(1, NZ):
            arrived(tb.at[:, (z + NZ - d) % NZ], tzr.at[d - 1])
        ones = jnp.ones((8, half), jnp.bfloat16)
        for b in range(NX):
            sq = jnp.square(tb[b].reshape(TILE, half).astype(jnp.float32))
            high = sq.astype(jnp.bfloat16)
            low = (sq - high.astype(jnp.float32)).astype(jnp.bfloat16)
            row = inner_rows(ones, high) + inner_rows(ones, low)
            for k in range(CH):
                pb[k, :, b, RZ:, :] = jnp.broadcast_to(row[None], (NY, 8, TILE))
        step = COLS // (NY * NZ)
        rows = lax.broadcasted_iota(jnp.int32, (COLS, COLS), 0)
        cols = lax.broadcasted_iota(jnp.int32, (COLS, COLS), 1)
        moved = (rows % TILE) // step * (NY * step) + rows // TILE * step + rows % step
        order[...] = jnp.where(moved == cols, 1.0, 0.0).astype(jnp.bfloat16)

    def owner_copy(k, dx, dy):
        tx, ty = (x + dx) % NX, (y + dy) % NY
        return remote(pb.at[k, ty, tx], fr.at[k % 2, y, x, c], es.at[k], ers.at[k % 2], dev(tx, ty, z, k // 2))

    def scores(k):
        for d in range(1, NY):
            arrived(fb.at[k, (y + NY - d) % NY], frs.at[k, d - 1])
        rows = fb[k].reshape(NY * RZ, half)
        high = rows.astype(jnp.bfloat16)
        low = (rows - high.astype(jnp.float32)).astype(jnp.bfloat16)
        both = inner_rows(jnp.concatenate([high, low], axis=0), tb[...].reshape(COLS, half))
        both = both[:NY * RZ] + both[NY * RZ:]
        sq = jnp.square(rows)
        high = sq.astype(jnp.bfloat16)
        low = (sq - high.astype(jnp.float32)).astype(jnp.bfloat16)
        ones = jnp.ones((8, half), jnp.bfloat16)
        norms = inner_rows(ones, high) + inner_rows(ones, low)
        for b in range(NX):
            pb[k, :, b, 0:RZ, :] = both[:, b * TILE:(b + 1) * TILE].reshape(NY, RZ, TILE)
            for a in range(NY):
                pb[k, a, b, RZ + 1:RZ + 2, 0:NY * RZ] = norms[0:1, :]
        same = c == k // 2

        @pl.when(same)
        def _():
            pltpu.make_async_copy(pb.at[k, y, x], fr.at[k % 2, y, x, c], ers.at[k % 2]).start()

        @pl.when(jnp.logical_not(same))
        def _():
            owner_copy(k, 0, 0).start()

        for dx in range(NX):
            for dy in range(NY):
                if dx or dy:
                    owner_copy(k, dx, dy).start()

    def forward(k):
        arrived(rows_of(k, left, 0), gr.at[k, 0])
        go([remote(rows_of(k, left, 0), rows_of(k, left, 0), gs.at[k, 4], gr.at[k, 4], dev(right, y, z, c))])
        arrived(rows_of(k, right, 1), gr.at[k, 2])
        go([remote(rows_of(k, right, 1), rows_of(k, right, 1), gs.at[k, 5], gr.at[k, 5], dev(left, y, z, c))])

    def dots(k):
        arrived(rows_of(k, left, 1), gr.at[k, 1])
        go([to_sibling(k, left, 1)])
        arrived(rows_of(k, right, 0), gr.at[k, 3])
        go([to_sibling(k, right, 2)])
        arrived(rows_of(k, across, 0), gr.at[k, 4])
        arrived(rows_of(k, across, 1), gr.at[k, 5])
        go([to_sibling(k, across, 3)])
        if k == 0:
            m_local.wait()
        own_product(k)
        if k == 0:
            arrived(mb.at[1], mr)
        arrived(gb.at[1, k, x], sr.at[k, 0])
        arrived(gb.at[1, k, left], sr.at[k, 1])
        arrived(gb.at[1, k, right], sr.at[k, 2])
        arrived(gb.at[1, k, across], sr.at[k, 3])
        for q in range(HP):
            sibling_product(k, q)
            y_send(k, q)

    def z_stages(k):
        for q in range(HP):
            z_stage(k, q)

    forward(0)
    forward(1)
    own_sends(2)
    dots(0)
    dots(1)
    forward(2)
    own_sends(3)
    target_squares()
    z_stages(0)
    forward(3)
    dots(2)
    z_stages(1)
    dots(3)
    z_stages(2)
    z_sum(0)
    z_sum(1)
    z_stages(3)
    scores(0)
    scores(1)
    z_sum(2)
    z_sum(3)
    scores(2)
    scores(3)

    for hh in range(2):
        arrived(fr.at[hh], ers.at[hh])
        blocks = []
        for b in range(NY):
            m = fr[hh, b, 0, 0]
            for q in range(1, NX * NC):
                m = m + fr[hh, b, q // NC, q % NC]
            blocks.append(m)
        m = jnp.concatenate(blocks, axis=1)
        parts = []
        for _ in range(3):
            parts.append(m.astype(jnp.bfloat16))
            m = m - parts[-1].astype(jnp.float32)
        m = jnp.dot(jnp.concatenate(parts, axis=0), order[...], preferred_element_type=jnp.float32)
        m = (m[0:2 * RZ] + m[2 * RZ:4 * RZ]) + m[4 * RZ:]
        row = lax.broadcasted_iota(jnp.int32, (RZ, TILE), 0)
        lane = lax.broadcasted_iota(jnp.int32, (RZ, TILE), 1)
        norms = jnp.broadcast_to(blocks[0][RZ + 1:RZ + 2, :], (RZ, TILE))
        fsq = jnp.sum(jnp.where(lane == y * RZ + row, norms, 0.0), axis=1, keepdims=True)
        out_ref[hh * RZ:(hh + 1) * RZ, :] = (
            float(K) ** 0.5
            * m[0:RZ]
            * lax.rsqrt(fsq + 1e-06)
            * lax.rsqrt(m[RZ:RZ + 1] + 1e-06)
        )

    for copy in started:
        copy.wait_send()
    for k in range(CH):
        def leave(block):
            remote(block, block, es.at[k], es.at[k], dev(x, y, z, sib)).wait_send()

        leave(pb.at[k, 0:NY - 1])
        leave(pb.at[k, 0, 0:NX - 1])

        @pl.when(c != k // 2)
        def _():
            leave(pb.at[k, 0, 0])
    for j in range(HP):
        for cc in range(NC):
            same, copy, source = deal(j, cc)

            @pl.when(jnp.logical_not(same))
            def _():
                copy.wait_send()


def per_device(grads, proj_matrix, targets):
    depth, dims = proj_matrix.shape
    half = dims // NC
    part = half // HP
    dma = pltpu.SemaphoreType.DMA
    bf16, f32 = jnp.bfloat16, jnp.float32
    return pl.pallas_call(
        kernel,
        out_shape=jax.ShapeDtypeStruct((2 * RZ, COLS), f32),
        in_specs=[pl.BlockSpec(memory_space=pltpu.HBM)] * 3,
        out_specs=pl.BlockSpec(memory_space=pltpu.VMEM),
        scratch_shapes=[
            pltpu.VMEM((NC, CH, NX, RC, depth), bf16),
            pltpu.VMEM((NC, depth, half), bf16),
            pltpu.VMEM((CH, HP, NY, RC, part), f32),
            pltpu.VMEM((CH, HP, NY, RC, part), bf16),
            pltpu.VMEM((CH, HP, NY - 1, RC, part), bf16),
            pltpu.VMEM((CH, HP, RC, part), f32),
            pltpu.VMEM((HP, RC, part), bf16),
            pltpu.VMEM((CH - 1, HP, NZ - 1, RZ, part), f32),
            pltpu.VMEM((HP, NZ - 1, RZ, part), bf16),
            pltpu.VMEM((CH, NY, RZ, half), f32),
            pltpu.VMEM((NY, NZ, targets.shape[0] // HP, half), bf16),
            pltpu.VMEM((COLS, COLS), bf16),
            pltpu.VMEM((CH, NY, NX, 2 * RZ, TILE), f32),
            pltpu.VMEM((2, NY, NX, NC, 2 * RZ, TILE), f32),
            dma((CH, NZ)), dma((2,)),
            dma((CH, 6)), dma((CH, 6)), dma((CH, 4)), dma((CH, 4)),
            dma, dma, dma((HP, NC)), dma,
            dma((NZ - 1,)), dma((NZ - 1,)),
            dma((CH, HP, NY - 1)), dma((CH, HP, NY - 1)),
            dma((CH, HP, NZ - 1)), dma((CH, HP, NZ - 1)),
            dma((CH, NY - 1)), dma((CH, NY - 1)),
            dma((CH,)), dma((2,)),
        ],
        compiler_params=pltpu.CompilerParams(
            collective_id=0, has_side_effects=True, vmem_limit_bytes=56 * 1024 * 1024
        ),
    )(grads, proj_matrix, targets)


def solution(mesh):
    placed = (P("grp", "proj"), P("proj", "grp"), P("proj", "grp"))
    return jax.shard_map(
        per_device, mesh=mesh, in_specs=placed, out_specs=P("proj", "grp"), check_vma=False
    )
```

```python
import jax
import jax.numpy as jnp
from jax import lax
from jax.experimental import pallas as pl
from jax.experimental.pallas import tpu as pltpu
from jax.sharding import PartitionSpec as P

K = 8192
MESH = pl.DeviceIdType.MESH
NX, NY, NZ, NC = 4, 4, 8, 2
CH, RC, RZ, HP = 4, 64, 8, 1
TJ = 2
COLS, TILE = 512, 128


def inner_rows(left, right):
    return lax.dot_general(
        left, right, (((1,), (1,)), ((), ())), preferred_element_type=jnp.float32
    )


def kernel(
    g_ref, m_ref, t_ref, out_ref,
    gb, mb, fo, fp, yr, zb, zq, zr, zt, fb, tb, order, pb, fr,
    gl, loc, gs, gr, ss, sr, ms, mr, ts, tr, tzs, tzr, ys, yrs, zs, zrs, fs, frs, es, ers,
):
    x = lax.axis_index("grp")
    p = lax.axis_index("proj")
    c = p % NC
    z = (p // NC) % NZ
    y = p // (NC * NZ)
    depth = m_ref.shape[0]
    half = m_ref.shape[1] // NC
    part = half // HP
    sib = 1 - c

    def dev(dx, dy, dz, dc):
        return ((dy * NZ + dz) * NC + dc, dx)

    right, left = (x + 1) % NX, (x + NX - 1) % NX
    across = (x + 2) % NX

    def remote(src, dst, send, recv, where):
        return pltpu.make_async_remote_copy(
            src_ref=src, dst_ref=dst, send_sem=send, recv_sem=recv,
            device_id=where, device_id_type=MESH,
        )

    def arrived(dst, sem):
        remote(dst, dst, sem, sem, dev(x, y, z, sib)).wait_recv()

    own_cols = pl.ds(pl.multiple_of(c * half, half), half)
    sib_cols = pl.ds(pl.multiple_of(sib * half, half), half)
    barrier = pltpu.get_barrier_semaphore()

    def greet(where):
        pl.semaphore_signal(barrier, inc=1, device_id=where, device_id_type=MESH)

    for d in range(1, NZ):
        greet(dev(x, y, (z + d) % NZ, c))
    for dx in range(NX):
        for dy in range(NY):
            for cs in range(NC):
                greet(dev((x + dx) % NX, (y + dy) % NY, z, cs))

    g_local = []
    for k in range(CH):
        g_local.append([
            pltpu.make_async_copy(
                g_ref.at[pl.ds(w * CH * RZ + k * RZ, RZ), :],
                gb.at[0, k, x, pl.ds(w * RZ, RZ), :], gl.at[k, w])
            for w in range(NZ)
        ])
    m_local = pltpu.make_async_copy(m_ref.at[:, own_cols], mb.at[0], loc.at[1])
    for k in range(CH):
        for copy in g_local[k]:
            copy.start()
    m_local.start()

    pl.semaphore_wait(barrier, NX * NY * NC + NZ - 1)

    started = []

    def go(copies):
        for copy in copies:
            copy.start()
            started.append(copy)

    def to_sibling(k, who, slot):
        return remote(gb.at[0, k, who], gb.at[1, k, who], ss.at[k, slot], sr.at[k, slot], dev(x, y, z, sib))

    def rows_of(k, who, which):
        return gb.at[0, k, who, pl.ds(which * (RC // 2), RC // 2), :]

    def own_sends(k):
        for copy in g_local[k]:
            copy.wait()
        first, last = rows_of(k, x, 0), rows_of(k, x, 1)
        go([
            remote(first, first, gs.at[k, 0], gr.at[k, 0], dev(right, y, z, c)),
            remote(last, last, gs.at[k, 2], gr.at[k, 2], dev(left, y, z, c)),
            remote(last, last, gs.at[k, 1], gr.at[k, 1], dev(right, y, z, c)),
            remote(first, first, gs.at[k, 3], gr.at[k, 3], dev(left, y, z, c)),
            to_sibling(k, x, 0),
        ])

    own_sends(0)
    trows = t_ref.shape[0] // TJ

    def deal(j, cc):
        source = t_ref.at[pl.ds(j * trows, trows), pl.ds(cc * half, half)]
        to = TJ * c + j
        same = (to == y) & (cc == c)
        return same, remote(source, tb.at[y, z], ts.at[j, cc], tr, dev(x, to, z, cc)), source

    for j in range(TJ):
        for cc in range(NC):
            same, copy, source = deal(j, cc)

            @pl.when(same)
            def _():
                pltpu.make_async_copy(source, tb.at[y, z], tr).start()

            @pl.when(jnp.logical_not(same))
            def _():
                copy.start()

    go([remote(m_ref.at[:, sib_cols], mb.at[1], ms, mr, dev(x, y, z, sib))])
    own_sends(1)

    arrived(tb.at[:, z], tr)
    for d in range(1, NZ):
        go([remote(tb.at[:, z], tb.at[:, z], tzs.at[d - 1], tzr.at[d - 1], dev(x, y, (z + d) % NZ, c))])

    def own_product(k):
        @pl.loop(0, half // 256)
        def _(n):
            cols = pl.ds(pl.multiple_of(n * 256, 256), 256)
            acc = jnp.dot(
                gb[0, k].reshape(NX * RC, depth), mb[0, :, cols], preferred_element_type=jnp.float32)
            fo[k, n // (part // 256), :, :, pl.ds(pl.multiple_of(n % (part // 256) * 256, 256), 256)] = (
                acc.reshape(NY, RC, 256))

    def sibling_product(k, h):
        @pl.loop(0, part // 256)
        def _(n):
            first = pl.multiple_of(n * 256, 256)
            cols = pl.ds(h * part + first, 256)
            acc = jnp.dot(
                gb[1, k].reshape(NX * RC, depth), mb[1, :, cols], preferred_element_type=jnp.float32)
            acc = fo[k, h, :, :, pl.ds(first, 256)] + acc.reshape(NY, RC, 256)
            fo[k, h, :, :, pl.ds(first, 256)] = acc
            fp[k, h, :, :, pl.ds(first, 256)] = acc.astype(jnp.bfloat16)

    def y_send(k, h):
        for d in range(1, NY):
            to = (y + d) % NY
            go([remote(fp.at[k, h, to], yr.at[k, h, d - 1], ys.at[k, h, d - 1], yrs.at[k, h, d - 1],
                       dev(x, to, z, c))])

    def z_slot(k, h, d):
        return zt.at[h, d - 1] if k == CH - 1 else zr.at[k, h, d - 1]

    def z_stage(k, h):
        for d in range(1, NY):
            arrived(yr.at[k, h, d - 1], yrs.at[k, h, d - 1])
        total = fo[k, h, y]
        for d in range(1, NY):
            total = total + yr[k, h, d - 1].astype(jnp.float32)
        zb[k, h] = total
        source = zb.at[k, h]
        if k == CH - 1:
            zq[h] = total.astype(jnp.bfloat16)
            source = zq.at[h]
        for d in range(1, NZ):
            to = (z + d) % NZ
            piece = pl.ds(pl.multiple_of(to * RZ, RZ), RZ)
            go([remote(source.at[piece, :], z_slot(k, h, d),
                       zs.at[k, h, d - 1], zrs.at[k, h, d - 1], dev(x, y, to, c))])

    def z_sum(k):
        for h in range(HP):
            for d in range(1, NZ):
                arrived(z_slot(k, h, d), zrs.at[k, h, d - 1])
            total = zb[k, h, pl.ds(pl.multiple_of(z * RZ, RZ), RZ), :]
            for d in range(1, NZ):
                total = total + z_slot(k, h, d)[...].astype(jnp.float32)
            fb[k, y, :, h * part:(h + 1) * part] = total
        for d in range(1, NY):
            to = (y + d) % NY
            go([remote(fb.at[k, y], fb.at[k, y], fs.at[k, d - 1], frs.at[k, d - 1], dev(x, to, z, c))])

    def target_squares():
        for d in range(1, NZ):
            arrived(tb.at[:, (z + NZ - d) % NZ], tzr.at[d - 1])
        ones = jnp.ones((8, half), jnp.bfloat16)
        for b in range(NX):
            sq = jnp.square(tb[b].reshape(TILE, half).astype(jnp.float32))
            high = sq.astype(jnp.bfloat16)
            low = (sq - high.astype(jnp.float32)).astype(jnp.bfloat16)
            row = inner_rows(ones, high) + inner_rows(ones, low)
            for k in range(CH):
                pb[k, :, b, RZ:, :] = jnp.broadcast_to(row[None], (NY, 8, TILE))
        step = COLS // (NY * NZ)
        rows = lax.broadcasted_iota(jnp.int32, (COLS, COLS), 0)
        cols = lax.broadcasted_iota(jnp.int32, (COLS, COLS), 1)
        moved = (rows % TILE) // step * (NY * step) + rows // TILE * step + rows % step
        order[...] = jnp.where(moved == cols, 1.0, 0.0).astype(jnp.bfloat16)

    def owner_copy(k, dx, dy):
        tx, ty = (x + dx) % NX, (y + dy) % NY
        return remote(pb.at[k, ty, tx], fr.at[k % 2, y, x, c], es.at[k], ers.at[k % 2], dev(tx, ty, z, k // 2))

    def scores(k):
        for d in range(1, NY):
            arrived(fb.at[k, (y + NY - d) % NY], frs.at[k, d - 1])
        rows = fb[k].reshape(NY * RZ, half)
        high = rows.astype(jnp.bfloat16)
        low = (rows - high.astype(jnp.float32)).astype(jnp.bfloat16)
        both = inner_rows(jnp.concatenate([high, low], axis=0), tb[...].reshape(COLS, half))
        both = both[:NY * RZ] + both[NY * RZ:]
        sq = jnp.square(rows)
        high = sq.astype(jnp.bfloat16)
        low = (sq - high.astype(jnp.float32)).astype(jnp.bfloat16)
        ones = jnp.ones((8, half), jnp.bfloat16)
        norms = inner_rows(ones, high) + inner_rows(ones, low)
        for b in range(NX):
            pb[k, :, b, 0:RZ, :] = both[:, b * TILE:(b + 1) * TILE].reshape(NY, RZ, TILE)
            for a in range(NY):
                pb[k, a, b, RZ + 1:RZ + 2, 0:NY * RZ] = norms[0:1, :]
        same = c == k // 2

        @pl.when(same)
        def _():
            pltpu.make_async_copy(pb.at[k, y, x], fr.at[k % 2, y, x, c], ers.at[k % 2]).start()

        @pl.when(jnp.logical_not(same))
        def _():
            owner_copy(k, 0, 0).start()

        for dx in range(NX):
            for dy in range(NY):
                if dx or dy:
                    owner_copy(k, dx, dy).start()

    def forward(k):
        arrived(rows_of(k, left, 0), gr.at[k, 0])
        go([remote(rows_of(k, left, 0), rows_of(k, left, 0), gs.at[k, 4], gr.at[k, 4], dev(right, y, z, c))])
        arrived(rows_of(k, right, 1), gr.at[k, 2])
        go([remote(rows_of(k, right, 1), rows_of(k, right, 1), gs.at[k, 5], gr.at[k, 5], dev(left, y, z, c))])

    def dots(k):
        arrived(rows_of(k, left, 1), gr.at[k, 1])
        go([to_sibling(k, left, 1)])
        arrived(rows_of(k, right, 0), gr.at[k, 3])
        go([to_sibling(k, right, 2)])
        arrived(rows_of(k, across, 0), gr.at[k, 4])
        arrived(rows_of(k, across, 1), gr.at[k, 5])
        go([to_sibling(k, across, 3)])
        if k == 0:
            m_local.wait()
        own_product(k)
        if k == 0:
            arrived(mb.at[1], mr)
        arrived(gb.at[1, k, x], sr.at[k, 0])
        arrived(gb.at[1, k, left], sr.at[k, 1])
        arrived(gb.at[1, k, right], sr.at[k, 2])
        arrived(gb.at[1, k, across], sr.at[k, 3])
        for q in range(HP):
            sibling_product(k, q)
            y_send(k, q)

    def z_stages(k):
        for q in range(HP):
            z_stage(k, q)

    forward(0)
    forward(1)
    own_sends(2)
    dots(0)
    dots(1)
    forward(2)
    own_sends(3)
    target_squares()
    z_stages(0)
    forward(3)
    dots(2)
    z_stages(1)
    dots(3)
    z_stages(2)
    z_sum(0)
    z_sum(1)
    z_stages(3)
    scores(0)
    scores(1)
    z_sum(2)
    z_sum(3)
    scores(2)
    scores(3)

    for copy in started:
        copy.wait_send()
    for j in range(TJ):
        for cc in range(NC):
            same, copy, source = deal(j, cc)

            @pl.when(jnp.logical_not(same))
            def _():
                copy.wait_send()

    for hh in range(2):
        arrived(fr.at[hh], ers.at[hh])
        blocks = []
        for b in range(NY):
            m = fr[hh, b, 0, 0]
            for q in range(1, NX * NC):
                m = m + fr[hh, b, q // NC, q % NC]
            blocks.append(m)
        m = jnp.concatenate(blocks, axis=1)
        parts = []
        for _ in range(3):
            parts.append(m.astype(jnp.bfloat16))
            m = m - parts[-1].astype(jnp.float32)
        m = jnp.dot(jnp.concatenate(parts, axis=0), order[...], preferred_element_type=jnp.float32)
        m = (m[0:2 * RZ] + m[2 * RZ:4 * RZ]) + m[4 * RZ:]
        row = lax.broadcasted_iota(jnp.int32, (RZ, TILE), 0)
        lane = lax.broadcasted_iota(jnp.int32, (RZ, TILE), 1)
        norms = jnp.broadcast_to(blocks[0][RZ + 1:RZ + 2, :], (RZ, TILE))
        fsq = jnp.sum(jnp.where(lane == y * RZ + row, norms, 0.0), axis=1, keepdims=True)
        out_ref[hh * RZ:(hh + 1) * RZ, :] = (
            float(K) ** 0.5
            * m[0:RZ]
            * lax.rsqrt(fsq + 1e-06)
            * lax.rsqrt(m[RZ:RZ + 1] + 1e-06)
        )

    for k in range(CH):
        def leave(block):
            remote(block, block, es.at[k], es.at[k], dev(x, y, z, sib)).wait_send()

        leave(pb.at[k, 0:NY - 1])
        leave(pb.at[k, 0, 0:NX - 1])

        @pl.when(c != k // 2)
        def _():
            leave(pb.at[k, 0, 0])

def per_device(grads, proj_matrix, targets):
    depth, dims = proj_matrix.shape
    half = dims // NC
    part = half // HP
    dma = pltpu.SemaphoreType.DMA
    bf16, f32 = jnp.bfloat16, jnp.float32
    return pl.pallas_call(
        kernel,
        out_shape=jax.ShapeDtypeStruct((2 * RZ, COLS), f32),
        in_specs=[pl.BlockSpec(memory_space=pltpu.HBM)] * 3,
        out_specs=pl.BlockSpec(memory_space=pltpu.VMEM),
        scratch_shapes=[
            pltpu.VMEM((NC, CH, NX, RC, depth), bf16),
            pltpu.VMEM((NC, depth, half), bf16),
            pltpu.VMEM((CH, HP, NY, RC, part), f32),
            pltpu.VMEM((CH, HP, NY, RC, part), bf16),
            pltpu.VMEM((CH, HP, NY - 1, RC, part), bf16),
            pltpu.VMEM((CH, HP, RC, part), f32),
            pltpu.VMEM((HP, RC, part), bf16),
            pltpu.VMEM((CH - 1, HP, NZ - 1, RZ, part), f32),
            pltpu.VMEM((HP, NZ - 1, RZ, part), bf16),
            pltpu.VMEM((CH, NY, RZ, half), f32),
            pltpu.VMEM((NY, NZ, targets.shape[0] // TJ, half), bf16),
            pltpu.VMEM((COLS, COLS), bf16),
            pltpu.VMEM((CH, NY, NX, 2 * RZ, TILE), f32),
            pltpu.VMEM((2, NY, NX, NC, 2 * RZ, TILE), f32),
            dma((CH, NZ)), dma((2,)),
            dma((CH, 6)), dma((CH, 6)), dma((CH, 4)), dma((CH, 4)),
            dma, dma, dma((TJ, NC)), dma,
            dma((NZ - 1,)), dma((NZ - 1,)),
            dma((CH, HP, NY - 1)), dma((CH, HP, NY - 1)),
            dma((CH, HP, NZ - 1)), dma((CH, HP, NZ - 1)),
            dma((CH, NY - 1)), dma((CH, NY - 1)),
            dma((CH,)), dma((2,)),
        ],
        compiler_params=pltpu.CompilerParams(
            collective_id=0, has_side_effects=True, vmem_limit_bytes=56 * 1024 * 1024
        ),
    )(grads, proj_matrix, targets)


def solution(mesh):
    placed = (P("grp", "proj"), P("proj", "grp"), P("proj", "grp"))
    return jax.shard_map(
        per_device, mesh=mesh, in_specs=placed, out_specs=P("proj", "grp"), check_vma=False
    )
```

```python
import jax
import jax.numpy as jnp
from jax import lax
from jax.experimental import pallas as pl
from jax.experimental.pallas import tpu as pltpu
from jax.sharding import PartitionSpec as P

K = 8192
MESH = pl.DeviceIdType.MESH
NX, NY, NZ, NC = 4, 4, 8, 2
CH, RC, RZ, HP = 4, 64, 8, 1
TJ = 2
COLS, TILE = 512, 128


def inner_rows(left, right):
    return lax.dot_general(
        left, right, (((1,), (1,)), ((), ())), preferred_element_type=jnp.float32
    )


def kernel(
    g_ref, m_ref, t_ref, out_ref,
    gb, mb, fo, fp, yr, zb, zq, zr, zt, fb, tb, order, pb, fr,
    gl, loc, gs, gr, ss, sr, ms, mr, ts, tr, tzs, tzr, ys, yrs, zs, zrs, fs, frs, es, ers,
):
    x = lax.axis_index("grp")
    p = lax.axis_index("proj")
    c = p % NC
    z = (p // NC) % NZ
    y = p // (NC * NZ)
    depth = m_ref.shape[0]
    half = m_ref.shape[1] // NC
    part = half // HP
    sib = 1 - c

    def dev(dx, dy, dz, dc):
        return ((dy * NZ + dz) * NC + dc, dx)

    right, left = (x + 1) % NX, (x + NX - 1) % NX
    across = (x + 2) % NX

    def remote(src, dst, send, recv, where):
        return pltpu.make_async_remote_copy(
            src_ref=src, dst_ref=dst, send_sem=send, recv_sem=recv,
            device_id=where, device_id_type=MESH,
        )

    def arrived(dst, sem):
        remote(dst, dst, sem, sem, dev(x, y, z, sib)).wait_recv()

    own_cols = pl.ds(pl.multiple_of(c * half, half), half)
    sib_cols = pl.ds(pl.multiple_of(sib * half, half), half)
    barrier = pltpu.get_barrier_semaphore()

    def greet(where):
        pl.semaphore_signal(barrier, inc=1, device_id=where, device_id_type=MESH)

    for d in range(1, NZ):
        greet(dev(x, y, (z + d) % NZ, c))
    for dx in range(NX):
        for dy in range(NY):
            for cs in range(NC):
                greet(dev((x + dx) % NX, (y + dy) % NY, z, cs))

    g_local = []
    for k in range(CH):
        g_local.append([
            pltpu.make_async_copy(
                g_ref.at[pl.ds(w * CH * RZ + k * RZ, RZ), :],
                gb.at[0, k, x, pl.ds(w * RZ, RZ), :], gl.at[k, w])
            for w in range(NZ)
        ])
    m_local = pltpu.make_async_copy(m_ref.at[:, own_cols], mb.at[0], loc.at[1])
    for k in range(CH):
        for copy in g_local[k]:
            copy.start()
    m_local.start()

    pl.semaphore_wait(barrier, NX * NY * NC + NZ - 1)

    started = []

    def go(copies):
        for copy in copies:
            copy.start()
            started.append(copy)

    def to_sibling(k, who, slot):
        return remote(gb.at[0, k, who], gb.at[1, k, who], ss.at[k, slot], sr.at[k, slot], dev(x, y, z, sib))

    def rows_of(k, who, which):
        return gb.at[0, k, who, pl.ds(which * (RC // 2), RC // 2), :]

    def own_sends(k):
        for copy in g_local[k]:
            copy.wait()
        first, last = rows_of(k, x, 0), rows_of(k, x, 1)
        go([
            remote(first, first, gs.at[k, 0], gr.at[k, 0], dev(right, y, z, c)),
            remote(last, last, gs.at[k, 2], gr.at[k, 2], dev(left, y, z, c)),
            remote(last, last, gs.at[k, 1], gr.at[k, 1], dev(right, y, z, c)),
            remote(first, first, gs.at[k, 3], gr.at[k, 3], dev(left, y, z, c)),
            to_sibling(k, x, 0),
        ])

    own_sends(0)
    trows = t_ref.shape[0] // TJ

    def deal(j, cc):
        source = t_ref.at[pl.ds(j * trows, trows), pl.ds(cc * half, half)]
        to = TJ * c + j
        same = (to == y) & (cc == c)
        return same, remote(source, tb.at[y, z], ts.at[j, cc], tr, dev(x, to, z, cc)), source

    for j in range(TJ):
        for cc in range(NC):
            same, copy, source = deal(j, cc)

            @pl.when(same)
            def _():
                pltpu.make_async_copy(source, tb.at[y, z], tr).start()

            @pl.when(jnp.logical_not(same))
            def _():
                copy.start()

    go([remote(m_ref.at[:, sib_cols], mb.at[1], ms, mr, dev(x, y, z, sib))])
    own_sends(1)

    arrived(tb.at[:, z], tr)
    for d in range(1, NZ):
        go([remote(tb.at[:, z], tb.at[:, z], tzs.at[d - 1], tzr.at[d - 1], dev(x, y, (z + d) % NZ, c))])

    def own_product(k):
        @pl.loop(0, half // 256)
        def _(n):
            cols = pl.ds(pl.multiple_of(n * 256, 256), 256)
            acc = jnp.dot(
                gb[0, k].reshape(NX * RC, depth), mb[0, :, cols], preferred_element_type=jnp.float32)
            fo[k, n // (part // 256), :, :, pl.ds(pl.multiple_of(n % (part // 256) * 256, 256), 256)] = (
                acc.reshape(NY, RC, 256))

    def sibling_product(k, h):
        @pl.loop(0, part // 256)
        def _(n):
            first = pl.multiple_of(n * 256, 256)
            cols = pl.ds(h * part + first, 256)
            acc = jnp.dot(
                gb[1, k].reshape(NX * RC, depth), mb[1, :, cols], preferred_element_type=jnp.float32)
            acc = fo[k, h, :, :, pl.ds(first, 256)] + acc.reshape(NY, RC, 256)
            fo[k, h, :, :, pl.ds(first, 256)] = acc
            fp[k, h, :, :, pl.ds(first, 256)] = acc.astype(jnp.bfloat16)

    def y_send(k, h):
        for d in range(1, NY):
            to = (y + d) % NY
            go([remote(fp.at[k, h, to], yr.at[k, h, d - 1], ys.at[k, h, d - 1], yrs.at[k, h, d - 1],
                       dev(x, to, z, c))])

    def z_slot(k, h, d):
        return zt.at[h, d - 1] if k == CH - 1 else zr.at[k, h, d - 1]

    def z_stage(k, h):
        for d in range(1, NY):
            arrived(yr.at[k, h, d - 1], yrs.at[k, h, d - 1])
        total = fo[k, h, y]
        for d in range(1, NY):
            total = total + yr[k, h, d - 1].astype(jnp.float32)
        zb[k, h] = total
        source = zb.at[k, h]
        if k == CH - 1:
            zq[h] = total.astype(jnp.bfloat16)
            source = zq.at[h]
        for d in (4, 3, 5, 2, 6, 1, 7):
            to = (z + d) % NZ
            piece = pl.ds(pl.multiple_of(to * RZ, RZ), RZ)
            go([remote(source.at[piece, :], z_slot(k, h, d),
                       zs.at[k, h, d - 1], zrs.at[k, h, d - 1], dev(x, y, to, c))])

    def z_sum(k):
        for h in range(HP):
            for d in range(1, NZ):
                arrived(z_slot(k, h, d), zrs.at[k, h, d - 1])
            total = zb[k, h, pl.ds(pl.multiple_of(z * RZ, RZ), RZ), :]
            for d in range(1, NZ):
                total = total + z_slot(k, h, d)[...].astype(jnp.float32)
            fb[k, y, :, h * part:(h + 1) * part] = total
        for d in range(1, NY):
            to = (y + d) % NY
            go([remote(fb.at[k, y], fb.at[k, y], fs.at[k, d - 1], frs.at[k, d - 1], dev(x, to, z, c))])

    def target_squares():
        for d in range(1, NZ):
            arrived(tb.at[:, (z + NZ - d) % NZ], tzr.at[d - 1])
        ones = jnp.ones((8, half), jnp.bfloat16)
        for b in range(NX):
            sq = jnp.square(tb[b].reshape(TILE, half).astype(jnp.float32))
            high = sq.astype(jnp.bfloat16)
            low = (sq - high.astype(jnp.float32)).astype(jnp.bfloat16)
            row = inner_rows(ones, high) + inner_rows(ones, low)
            for k in range(CH):
                pb[k, :, b, RZ:, :] = jnp.broadcast_to(row[None], (NY, 8, TILE))
        step = COLS // (NY * NZ)
        rows = lax.broadcasted_iota(jnp.int32, (COLS, COLS), 0)
        cols = lax.broadcasted_iota(jnp.int32, (COLS, COLS), 1)
        moved = (rows % TILE) // step * (NY * step) + rows // TILE * step + rows % step
        order[...] = jnp.where(moved == cols, 1.0, 0.0).astype(jnp.bfloat16)

    def owner_copy(k, dx, dy):
        tx, ty = (x + dx) % NX, (y + dy) % NY
        return remote(pb.at[k, ty, tx], fr.at[k % 2, y, x, c], es.at[k], ers.at[k % 2], dev(tx, ty, z, k // 2))

    def scores(k):
        for d in range(1, NY):
            arrived(fb.at[k, (y + NY - d) % NY], frs.at[k, d - 1])
        rows = fb[k].reshape(NY * RZ, half)
        high = rows.astype(jnp.bfloat16)
        low = (rows - high.astype(jnp.float32)).astype(jnp.bfloat16)
        both = inner_rows(jnp.concatenate([high, low], axis=0), tb[...].reshape(COLS, half))
        both = both[:NY * RZ] + both[NY * RZ:]
        sq = jnp.square(rows)
        high = sq.astype(jnp.bfloat16)
        low = (sq - high.astype(jnp.float32)).astype(jnp.bfloat16)
        ones = jnp.ones((8, half), jnp.bfloat16)
        norms = inner_rows(ones, high) + inner_rows(ones, low)
        for b in range(NX):
            pb[k, :, b, 0:RZ, :] = both[:, b * TILE:(b + 1) * TILE].reshape(NY, RZ, TILE)
            for a in range(NY):
                pb[k, a, b, RZ + 1:RZ + 2, 0:NY * RZ] = norms[0:1, :]
        for dx in (2, 1, 3, 0):
            for dy in (2, 1, 3, 0):
                if dx or dy:
                    owner_copy(k, dx, dy).start()

        same = c == k // 2

        @pl.when(same)
        def _():
            pltpu.make_async_copy(pb.at[k, y, x], fr.at[k % 2, y, x, c], ers.at[k % 2]).start()

        @pl.when(jnp.logical_not(same))
        def _():
            owner_copy(k, 0, 0).start()

    def forward(k):
        arrived(rows_of(k, left, 0), gr.at[k, 0])
        go([remote(rows_of(k, left, 0), rows_of(k, left, 0), gs.at[k, 4], gr.at[k, 4], dev(right, y, z, c))])
        arrived(rows_of(k, right, 1), gr.at[k, 2])
        go([remote(rows_of(k, right, 1), rows_of(k, right, 1), gs.at[k, 5], gr.at[k, 5], dev(left, y, z, c))])

    def dots(k):
        arrived(rows_of(k, left, 1), gr.at[k, 1])
        go([to_sibling(k, left, 1)])
        arrived(rows_of(k, right, 0), gr.at[k, 3])
        go([to_sibling(k, right, 2)])
        arrived(rows_of(k, across, 0), gr.at[k, 4])
        arrived(rows_of(k, across, 1), gr.at[k, 5])
        go([to_sibling(k, across, 3)])
        if k == 0:
            m_local.wait()
        own_product(k)
        if k == 0:
            arrived(mb.at[1], mr)
        arrived(gb.at[1, k, x], sr.at[k, 0])
        arrived(gb.at[1, k, left], sr.at[k, 1])
        arrived(gb.at[1, k, right], sr.at[k, 2])
        arrived(gb.at[1, k, across], sr.at[k, 3])
        for q in range(HP):
            sibling_product(k, q)
            y_send(k, q)

    def z_stages(k):
        for q in range(HP):
            z_stage(k, q)

    forward(0)
    forward(1)
    own_sends(2)
    dots(0)
    dots(1)
    forward(2)
    own_sends(3)
    target_squares()
    z_stages(0)
    forward(3)
    dots(2)
    z_stages(1)
    dots(3)
    z_stages(2)
    z_sum(0)
    z_sum(1)
    z_stages(3)
    scores(0)
    scores(1)
    z_sum(2)
    z_sum(3)
    scores(2)
    scores(3)

    for copy in started:
        copy.wait_send()
    for j in range(TJ):
        for cc in range(NC):
            same, copy, source = deal(j, cc)

            @pl.when(jnp.logical_not(same))
            def _():
                copy.wait_send()

    for hh in range(2):
        arrived(fr.at[hh], ers.at[hh])
        blocks = []
        for b in range(NY):
            m = fr[hh, b, 0, 0]
            for q in range(1, NX * NC):
                m = m + fr[hh, b, q // NC, q % NC]
            blocks.append(m)
        m = jnp.concatenate(blocks, axis=1)
        parts = []
        for _ in range(3):
            parts.append(m.astype(jnp.bfloat16))
            m = m - parts[-1].astype(jnp.float32)
        m = jnp.dot(jnp.concatenate(parts, axis=0), order[...], preferred_element_type=jnp.float32)
        m = (m[0:2 * RZ] + m[2 * RZ:4 * RZ]) + m[4 * RZ:]
        row = lax.broadcasted_iota(jnp.int32, (RZ, TILE), 0)
        lane = lax.broadcasted_iota(jnp.int32, (RZ, TILE), 1)
        norms = jnp.broadcast_to(blocks[0][RZ + 1:RZ + 2, :], (RZ, TILE))
        fsq = jnp.sum(jnp.where(lane == y * RZ + row, norms, 0.0), axis=1, keepdims=True)
        out_ref[hh * RZ:(hh + 1) * RZ, :] = (
            float(K) ** 0.5
            * m[0:RZ]
            * lax.rsqrt(fsq + 1e-06)
            * lax.rsqrt(m[RZ:RZ + 1] + 1e-06)
        )

    for k in range(CH):
        def leave(block):
            remote(block, block, es.at[k], es.at[k], dev(x, y, z, sib)).wait_send()

        leave(pb.at[k, 0:NY - 1])
        leave(pb.at[k, 0, 0:NX - 1])

        @pl.when(c != k // 2)
        def _():
            leave(pb.at[k, 0, 0])

def per_device(grads, proj_matrix, targets):
    depth, dims = proj_matrix.shape
    half = dims // NC
    part = half // HP
    dma = pltpu.SemaphoreType.DMA
    bf16, f32 = jnp.bfloat16, jnp.float32
    return pl.pallas_call(
        kernel,
        out_shape=jax.ShapeDtypeStruct((2 * RZ, COLS), f32),
        in_specs=[pl.BlockSpec(memory_space=pltpu.HBM)] * 3,
        out_specs=pl.BlockSpec(memory_space=pltpu.VMEM),
        scratch_shapes=[
            pltpu.VMEM((NC, CH, NX, RC, depth), bf16),
            pltpu.VMEM((NC, depth, half), bf16),
            pltpu.VMEM((CH, HP, NY, RC, part), f32),
            pltpu.VMEM((CH, HP, NY, RC, part), bf16),
            pltpu.VMEM((CH, HP, NY - 1, RC, part), bf16),
            pltpu.VMEM((CH, HP, RC, part), f32),
            pltpu.VMEM((HP, RC, part), bf16),
            pltpu.VMEM((CH - 1, HP, NZ - 1, RZ, part), f32),
            pltpu.VMEM((HP, NZ - 1, RZ, part), bf16),
            pltpu.VMEM((CH, NY, RZ, half), f32),
            pltpu.VMEM((NY, NZ, targets.shape[0] // TJ, half), bf16),
            pltpu.VMEM((COLS, COLS), bf16),
            pltpu.VMEM((CH, NY, NX, 2 * RZ, TILE), f32),
            pltpu.VMEM((2, NY, NX, NC, 2 * RZ, TILE), f32),
            dma((CH, NZ)), dma((2,)),
            dma((CH, 6)), dma((CH, 6)), dma((CH, 4)), dma((CH, 4)),
            dma, dma, dma((TJ, NC)), dma,
            dma((NZ - 1,)), dma((NZ - 1,)),
            dma((CH, HP, NY - 1)), dma((CH, HP, NY - 1)),
            dma((CH, HP, NZ - 1)), dma((CH, HP, NZ - 1)),
            dma((CH, NY - 1)), dma((CH, NY - 1)),
            dma((CH,)), dma((2,)),
        ],
        compiler_params=pltpu.CompilerParams(
            collective_id=0, has_side_effects=True, vmem_limit_bytes=56 * 1024 * 1024
        ),
    )(grads, proj_matrix, targets)


def solution(mesh):
    placed = (P("grp", "proj"), P("proj", "grp"), P("proj", "grp"))
    return jax.shard_map(
        per_device, mesh=mesh, in_specs=placed, out_specs=P("proj", "grp"), check_vma=False
    )
```
